256 devices in a mesh: dp: 16 (over x, y), expert: 16 (over z, core).
Axes of the slice: x: 4, y: 4, z: 8, core: 2. Of those that a mesh axis runs over, the one named last changes fastest.
Arguments:
- hidden: bfloat16 [16, 16, 384, 1024], P('dp', 'expert'), may hold values from -6 to 6
- down_weight: bfloat16 [16, 1024, 3584], P('expert'), may hold values from -0.1875 to 0.1875
- cotangent: bfloat16 [8192, 3584], P('dp', 'expert'), may hold values from -6 to 6
- expert_ids: int32 [8192, 8], P('dp'), may hold values from 0 to 15, as said below
- gate_weights: bfloat16 [8192, 8], P('dp'), may hold values from 0.049804688 to 0.5
- row_token: int32 [16, 16, 384], P('dp', 'expert'), may hold values from -1 to 511, as said below
- tile_count: int32 [16, 16], P('dp', 'expert'), may hold values from 1 to 3, as said below
Outputs:
- mixed_out: bfloat16 [8192, 3584], P('dp', 'expert')
- hidden_grad: bfloat16 [16, 16, 384, 1024], P('dp', 'expert')
- weight_grad: float32 [16, 1024, 3584], P('expert', 'dp')
The draws below stay inside these ranges and needn't reach their ends.
Inputs may be any that keep to these rules, and one draw needn't show every extreme that they name: `expert_ids`: each token names 8 different experts; every expert is named by some token of every group. row_token[i, e, r] is the index within group i (0 to 511) of a token that names expert e, or -1 for an empty slot; each token of a group stands exactly once in the rows of each expert it names and nowhere else; an expert's filled rows come first. tile_count[i, e] is the number of 128-row tiles that hold expert e's filled rows in group i, except for one expert of every group whose count is one tile less; the busiest expert of every group has 384 filled rows, all of them counted.
All inputs are finite; a program needn't handle non-finite values.
Results may differ from the reference program's by a relative error of at most 0.013.
Values may be sent and summed in bfloat16 or wider, within the bound.
A program may use at most 128 MiB of HBM per device.

```python
import math
import jax
import jax.numpy as jnp
from jax import lax

D = 3584
H = 1024
TOPK = 8
EXPERTS = 16
TILE = 128
GROUP_TOK = 512
TOKENS = 8192
MEAN_ROWS = 256
ROWS_CAP = 384
N_DP = 16


def group_plan(group_key):
    pair_order = jax.random.permutation(jax.random.fold_in(group_key, 11), EXPERTS)
    half_mean = MEAN_ROWS // 2
    shifts = jax.random.randint(jax.random.fold_in(group_key, 12), (EXPERTS // 2,), 0, half_mean + 1)
    shifts = shifts.at[0].set(half_mean)
    signed = jnp.stack([shifts, -shifts], axis=1).reshape(EXPERTS)
    loads = jnp.zeros((EXPERTS,), jnp.int32).at[pair_order].set(MEAN_ROWS + signed)
    ends = jnp.cumsum(loads)
    starts = ends - loads
    positions = jnp.arange(GROUP_TOK * TOPK, dtype=jnp.int32)
    owner_expert = jnp.sum((positions[:, None] >= ends[None, :]).astype(jnp.int32), axis=1)
    token_perm = jax.random.permutation(jax.random.fold_in(group_key, 13), GROUP_TOK).astype(jnp.int32)
    by_column = owner_expert.reshape(TOPK, GROUP_TOK).T
    ids_group = jnp.zeros((GROUP_TOK, TOPK), jnp.int32).at[token_perm].set(by_column)
    slot_index = jnp.arange(ROWS_CAP, dtype=jnp.int32)
    flat_pos = starts[:, None] + slot_index[None, :]
    rows_group = jnp.where(slot_index[None, :] < loads[:, None], token_perm[flat_pos % GROUP_TOK], -1)
    needed = (loads + TILE - 1) // TILE
    last_fill = loads - TILE * (needed - 1)
    expert_index = jnp.arange(EXPERTS, dtype=jnp.int32)
    eligible = (needed >= 2) & (expert_index != pair_order[0])
    score = jnp.where(eligible, last_fill * EXPERTS + expert_index, -1)
    short_expert = jnp.argmax(score)
    counts_group = needed - (expert_index == short_expert).astype(jnp.int32)
    return (ids_group, rows_group.astype(jnp.int32), counts_group.astype(jnp.int32))


def all_groups(key):
    base_key = jax.random.fold_in(key, 5)
    group_keys = jax.vmap(lambda index: jax.random.fold_in(base_key, index))(jnp.arange(N_DP))
    return jax.vmap(group_plan)(group_keys)


def draw_expert_ids(key, part):
    return all_groups(key)[0].reshape(TOKENS, TOPK)


def draw_row_token(key, part):
    return all_groups(key)[1]


def draw_tile_count(key, part):
    return all_groups(key)[2]


def level_of(stream_key, extent, cuts, smallest, largest):
    gain = 1.0
    for dim, shards_of in cuts:
        draws = jax.random.uniform(jax.random.fold_in(jax.random.fold_in(stream_key, 6), dim), (shards_of,), jnp.float32, smallest / len(cuts), largest / len(cuts))
        gain = gain * jnp.repeat(jnp.exp(draws), extent[dim] // shards_of).reshape((-1,) + (1,) * (len(extent) - 1 - dim))
    return gain


def scatter_about(rng, shape, spread, bound, shards=(), kind=jnp.bfloat16):
    gain = level_of(rng, shape, shards, -0.22, 0.18) if shards else 1.0
    array = jax.random.normal(rng, shape, jnp.float32) * spread * gain
    return jnp.minimum(jnp.maximum(array, -bound), bound).astype(kind)


def setup_inputs(seed: int = 0) -> dict:
    key_list = jax.random.split(jax.random.key(seed), 8)
    hidden = scatter_about(key_list[0], (N_DP, EXPERTS, ROWS_CAP, H), 1.0, 6.0, ((0, 16), (1, 16)))
    down_weight = scatter_about(key_list[1], (EXPERTS, H, D), H ** -0.5, 0.1875, ((0, 16),))
    cotangent = scatter_about(key_list[2], (TOKENS, D), 1.0, 6.0, ((0, 16), (1, 16)))
    expert_ids = draw_expert_ids(jax.random.fold_in(key_list[7], 71), 0)
    gate_weights = jnp.clip(jnp.exp(math.log(0.5) - 2.306499 * jax.random.uniform(key_list[4], (TOKENS, TOPK), jnp.float32) ** level_of(key_list[4], (TOKENS, TOPK), ((0, 16),), -0.2, 0.2)), 0.049804688, 0.5).astype(jnp.bfloat16)
    row_token = draw_row_token(jax.random.fold_in(key_list[7], 71), 0)
    tile_count = draw_tile_count(jax.random.fold_in(key_list[7], 71), 0)
    return dict(hidden=hidden, down_weight=down_weight, cotangent=cotangent, expert_ids=expert_ids, gate_weights=gate_weights, row_token=row_token, tile_count=tile_count)


def group_terms(hidden_rows, down_weight, token_rows, counts, group_ids, group_gates, group_cotangent):
    slot_index = jnp.arange(ROWS_CAP, dtype=jnp.int32)
    expert_index = jnp.arange(EXPERTS, dtype=jnp.int32)
    live_rows = (token_rows >= 0) & (slot_index[None, :] < counts[:, None] * TILE)
    safe_rows = jnp.where(live_rows, token_rows, 0).astype(jnp.int32)
    named_here = group_ids[safe_rows] == expert_index[:, None, None]
    row_gate = jnp.sum(jnp.where(named_here, group_gates[safe_rows].astype(jnp.float32), 0.0), axis=-1)
    row_gate = jnp.where(live_rows, row_gate, 0.0)
    weight_full = down_weight.astype(jnp.float32)
    hidden_full = hidden_rows.astype(jnp.float32)
    out_rows = jnp.einsum("erh,ehd->erd", hidden_full, weight_full).astype(jnp.bfloat16)
    contrib = row_gate[:, :, None] * out_rows.astype(jnp.float32)
    target = jnp.where(live_rows, token_rows, GROUP_TOK).astype(jnp.int32).reshape(-1)
    mixed_group = jnp.zeros((GROUP_TOK, D), jnp.float32).at[target].add(contrib.reshape(-1, D), mode="drop")
    routed = (row_gate[:, :, None] * group_cotangent[safe_rows].astype(jnp.float32)).astype(jnp.bfloat16)
    routed_full = routed.astype(jnp.float32)
    hidden_grad = jnp.einsum("erd,ehd->erh", routed_full, weight_full).astype(jnp.bfloat16)
    weight_part = jnp.einsum("erh,erd->ehd", hidden_full, routed_full).astype(jnp.bfloat16)
    return mixed_group.astype(jnp.bfloat16), hidden_grad, weight_part


def reference(hidden, down_weight, cotangent, expert_ids, gate_weights, row_token, tile_count):
    ids_groups = expert_ids.reshape(N_DP, GROUP_TOK, TOPK)
    gate_groups = gate_weights.reshape(N_DP, GROUP_TOK, TOPK)
    cot_groups = cotangent.reshape(N_DP, GROUP_TOK, D)

    def scan_group(grad_total, inputs):
        mixed_group, hidden_grad, weight_part = group_terms(inputs[0], down_weight, inputs[1], inputs[2], inputs[3], inputs[4], inputs[5])
        return grad_total + weight_part.astype(jnp.float32), (mixed_group, hidden_grad)

    grad_total, outputs = lax.scan(scan_group, jnp.zeros((EXPERTS, H, D), jnp.float32), (hidden, row_token, tile_count, ids_groups, gate_groups, cot_groups))
    return outputs[0].reshape(TOKENS, D), outputs[1], grad_total
```

```python
import jax
import jax.numpy as jnp
from jax import lax
from jax.experimental import pallas as pl
from jax.experimental.pallas import tpu as pltpu
from jax.sharding import PartitionSpec as P

MESH = pl.DeviceIdType.MESH
ROWS, HID, DIM, TOK = 384, 1024, 3584, 512
NZ = 8
BLK, SUB, ZBL, PAIR = 224, 112, 448, 896
WIDTHS = (512, 896, 896, 896, 512)
NT = (((1,), (1,)), ((), ()))
NN = (((1,), (0,)), ((), ()))
TN = (((0,), (0,)), ((), ()))
BF, F32 = jnp.bfloat16, jnp.float32
N_COPIES = 128


def dot(a, b, dims):
    return lax.dot_general(a, b, dims, preferred_element_type=F32)


def eye(n):
    return (
        lax.broadcasted_iota(jnp.int32, (n, n), 0) == lax.broadcasted_iota(jnp.int32, (n, n), 1)
    ).astype(F32).astype(BF)


def kernel(*refs):
    (hid_h, w_h, cot_h, ids_h, gw_h, tok_h, cnt_s, mix_o, hg_o, wg_o) = refs[:10]
    it = iter(refs[10:])
    nxt = lambda: next(it)
    hid, hT, hP, w, cot, ids, gw, tok, GT, cotT, RT = (nxt() for _ in range(11))
    PB = [nxt() for _ in range(5)]
    RF = [nxt() for _ in range(5)]
    RN = [nxt() for _ in range(5)]
    S2 = [nxt() for _ in range(5)]
    RF2 = [nxt() for _ in range(5)]
    RN2 = [nxt() for _ in range(5)]
    FB = [nxt() for _ in range(5)]
    OZ, wgb, M, MR, ZS, ZR, acc, hgb, mixb, mixT = (nxt() for _ in range(10))
    send_sem, recv_sem, loc_sem = (nxt() for _ in range(3))

    dpi, ei = lax.axis_index("dp"), lax.axis_index("expert")
    x, y, z, c = dpi // 4, dpi % 4, ei // 2, ei % 2
    m1 = (1 - c) * x + c * y
    m2 = (1 - c) * y + c * x

    def dpid(p1, p2):
        return (1 - c) * (p1 * 4 + p2) + c * (p2 * 4 + p1)

    def zz(s):
        return (z + s + NZ) % NZ

    n1p = (dpid((m1 + 1) % 4, m2), ei)
    n1m = (dpid((m1 + 3) % 4, m2), ei)
    n2p = (dpid(m1, (m2 + 1) % 4), ei)
    n2m = (dpid(m1, (m2 + 3) % 4), ei)
    zp = (dpi, zz(1) * 2 + c)
    zm = (dpi, zz(-1) * 2 + c)
    pt = (dpi, z * 2 + 1 - c)

    loads = {}

    def load(name, src, dst):
        cp = pltpu.make_async_copy(src, dst, loc_sem.at[len(loads)])
        cp.start()
        loads[name] = cp

    load("cot", cot_h, cot)
    load("ids", ids_h, ids)
    load("gw", gw_h, gw)
    load("tok", tok_h, tok)
    load("hid", hid_h, hid)
    for p in range(4):
        load(f"w{p}", w_h.at[:, pl.ds(p * PAIR, PAIR)], w.at[:, pl.ds(p * PAIR, PAIR)])

    barrier = pltpu.get_barrier_semaphore()
    for dev in (n1p, n1m, n2p, n2m, zp, zm, pt):
        pl.semaphore_signal(barrier, inc=1, device_id=dev, device_id_type=MESH)

    copies = {}

    def send(key, src, dst, dev):
        k = len(copies)
        cp = pltpu.make_async_remote_copy(
            src_ref=src,
            dst_ref=dst,
            send_sem=send_sem.at[k],
            recv_sem=recv_sem.at[k],
            device_id=dev,
            device_id_type=MESH,
        )
        cp.start()
        copies[key] = cp

    def got(*key):
        copies[key].wait_recv()

    def crow(s, core, sub, n=SUB):
        return cotT.at[pl.ds(pl.multiple_of(zz(s) * ZBL + core * BLK + sub * SUB, 16), n)]

    loads["cot"].wait()
    own_row = pl.multiple_of(z * ZBL + c * BLK, 16)
    cotT[pl.ds(own_row, BLK), :] = dot(eye(BLK), cot[...], NT).astype(BF)
    pl.semaphore_wait(barrier, 7)
    send(("p", 0), crow(0, c, 0, BLK), crow(0, c, 0, BLK), pt)
    for sub in range(2):
        send(("u", 0, sub), crow(0, c, sub), crow(0, c, sub), zp)
        send(("d", 0, sub), crow(0, c, sub), crow(0, c, sub), zm)

    loads["ids"].wait()
    loads["gw"].wait()
    loads["tok"].wait()
    gate_col = jnp.sum(
        jnp.where(ids[...] == ei, gw[...].astype(F32), 0.0), axis=1, keepdims=True
    )
    it_t = lax.broadcasted_iota(jnp.int32, (TOK, ROWS), 0)
    it_r = lax.broadcasted_iota(jnp.int32, (TOK, ROWS), 1)
    live = (tok[...] == it_t) & (it_r < cnt_s[0, 0] * 128)
    gates = jnp.where(live, gate_col, 0.0).astype(BF)
    GT[...] = dot(eye(ROWS), gates, NT).astype(BF)

    loads["hid"].wait()
    for j in range(4):
        hT[256 * j : 256 * j + 256, :] = dot(
            eye(256), hid[:, 256 * j : 256 * j + 256], NT
        ).astype(BF)
    for r1 in range(4):
        for r2 in range(4):
            row = pl.multiple_of(64 * dpid((m1 + r1) % 4, (m2 + r2) % 4), 64)
            o = (r1 * 4 + r2) * 64
            hP[o : o + 64, :] = hT[pl.ds(row, 64), :]

    def ag(s, sub):
        got("u", s - 1, sub)
        src = crow(-s, c, sub)
        if s <= 2 or (s == 3 and sub == 0):
            send(("u", s, sub), src, src, zp)
        send(("pu", s, sub), src, src, pt)
        got("d", s - 1, sub)
        src = crow(s, c, sub)
        if s <= 2 or (s == 3 and sub == 1):
            send(("d", s, sub), src, src, zm)
        send(("pd", s, sub), src, src, pt)

    def ag_last():
        got("u", 3, 0)
        src = crow(-4, c, 0)
        send(("pu", 4, 0), src, src, pt)
        got("d", 3, 1)
        src = crow(4, c, 1)
        send(("pd", 4, 1), src, src, pt)

    def zrows(s):
        return cotT[pl.ds(pl.multiple_of(zz(s) * ZBL, 16), ZBL), :]

    def x1(k):
        if k == 0:
            got("p", 0)
        elif k == 4:
            got("pu", 4, 0)
            got("pd", 4, 1)
        else:
            for sub in range(2):
                got("pu", k, sub)
                got("pd", k, sub)
        wd = WIDTHS[k]
        if k in (0, 4):
            rows = jnp.concatenate([zrows(k), jnp.zeros((64, TOK), BF)], axis=0)
        else:
            rows = jnp.concatenate([zrows(k), zrows(-k)], axis=0)
        RT[:, 0:wd] = dot(GT[...], rows, NT).astype(BF)
        pb, rf, rn = PB[k], RF[k], RN[k]
        for r1 in (2, 1, 3, 0):
            pb[r1] = dot(hP[256 * r1 : 256 * r1 + 256, :], RT[:, 0:wd], NN).astype(BF)
            if r1 == 2:
                send(("F+", k), pb.at[2, pl.ds(0, 128)], rf.at[0], n1p)
                send(("F-", k), pb.at[2, pl.ds(128, 128)], rf.at[1], n1m)
            elif r1 == 1:
                send(("N+b", k), pb.at[1, pl.ds(128, 128)], rn.at[0, pl.ds(128, 128)], n1p)
            elif r1 == 3:
                send(("N-a", k), pb.at[3, pl.ds(0, 128)], rn.at[1, pl.ds(0, 128)], n1m)

    def x1b(k):
        pb, rf, rn = PB[k], RF[k], RN[k]
        got("F+", k)
        pb[1, 0:128, :] = (pb[1, 0:128, :].astype(F32) + rf[0].astype(F32)).astype(BF)
        send(("N+a", k), pb.at[1, pl.ds(0, 128)], rn.at[0, pl.ds(0, 128)], n1p)
        got("F-", k)
        pb[3, 128:256, :] = (pb[3, 128:256, :].astype(F32) + rf[1].astype(F32)).astype(BF)
        send(("N-b", k), pb.at[3, pl.ds(128, 128)], rn.at[1, pl.ds(128, 128)], n1m)

    def x2(k):
        pb, rn, s2, rf2, rn2 = PB[k], RN[k], S2[k], RF2[k], RN2[k]
        for key in ("N+b", "N-a", "N+a", "N-b"):
            got(key, k)
        for r2 in (2, 1, 3, 0):
            sl = slice(64 * r2, 64 * r2 + 64)
            tot = pb[0, sl, :].astype(F32) + rn[0, sl, :].astype(F32) + rn[1, sl, :].astype(F32)
            if r2 == 0:
                FB[k][...] = tot
            else:
                s2[r2] = tot.astype(BF)
            if r2 == 2:
                send(("f+", k), s2.at[2, pl.ds(0, 32)], rf2.at[0], n2p)
                send(("f-", k), s2.at[2, pl.ds(32, 32)], rf2.at[1], n2m)
            elif r2 == 1:
                send(("n+b", k), s2.at[1, pl.ds(32, 32)], rn2.at[0, pl.ds(32, 32)], n2p)
            elif r2 == 3:
                send(("n-a", k), s2.at[3, pl.ds(0, 32)], rn2.at[1, pl.ds(0, 32)], n2m)

    def x2b(k):
        s2, rf2, rn2 = S2[k], RF2[k], RN2[k]
        got("f+", k)
        s2[1, 0:32, :] = (s2[1, 0:32, :].astype(F32) + rf2[0].astype(F32)).astype(BF)
        send(("n+a", k), s2.at[1, pl.ds(0, 32)], rn2.at[0, pl.ds(0, 32)], n2p)
        got("f-", k)
        s2[3, 32:64, :] = (s2[3, 32:64, :].astype(F32) + rf2[1].astype(F32)).astype(BF)
        send(("n-b", k), s2.at[3, pl.ds(32, 32)], rn2.at[1, pl.ds(32, 32)], n2m)

    def x3(k):
        rn2 = RN2[k]
        for key in ("n+b", "n-a", "n+a", "n-b"):
            got(key, k)
        tot = FB[k][...] + rn2[0].astype(F32) + rn2[1].astype(F32)
        OZ[zz(k)] = tot[:, 0:512]
        if k in (1, 2, 3):
            OZ[zz(-k)] = pltpu.roll(tot[:, 384:896], 448, 1)

    def mixed(p):
        loads[f"w{p}"].wait()
        out = dot(hid[...], w[:, PAIR * p : PAIR * p + PAIR], NN).astype(BF)
        mt = dot(out, GT[...], TN).astype(BF)
        for k in range(2):
            for cc in range(2):
                o = ZBL * k + BLK * cc
                M[cc, 2 * p + k] = mt[o : o + BLK, :]
        send(("m", p), M.at[1 - c, pl.ds(2 * p, 2)], MR.at[pl.ds(2 * p, 2)], pt)

    def both(t, sl):
        return M[c, t, sl, :].astype(F32) + MR[t, sl, :].astype(F32)

    def rz(k):
        if k == 1:
            for p in range(4):
                got("m", p)
        for sub in range(2):
            sl = slice(SUB * sub, SUB * sub + SUB)
            for dirn, dev in ((0, zp), (1, zm)):
                if k == 1 and sub != dirn:
                    continue
                t = zz(5 - k) if dirn == 0 else zz(k - 5)
                v = both(t, sl)
                if k >= 3 or (k == 2 and sub == dirn):
                    got("z", dirn, k - 1, sub)
                    v = v + ZR[dirn, k - 2, sl, :].astype(F32)
                ZS[dirn, k - 1, sl, :] = v.astype(BF)
                send(
                    ("z", dirn, k, sub),
                    ZS.at[dirn, k - 1, pl.ds(SUB * sub, SUB)],
                    ZR.at[dirn, k - 1, pl.ds(SUB * sub, SUB)],
                    dev,
                )

    stores = []

    def store(src, dst):
        cp = pltpu.make_async_copy(src, dst, loc_sem.at[len(loads) + len(stores)])
        cp.start()
        stores.append(cp)

    def rz_last():
        for sub in range(2):
            for dirn in range(2):
                got("z", dirn, 4, sub)
        v = both(z, slice(0, BLK)) + ZR[0, 3].astype(F32) + ZR[1, 3].astype(F32)
        mixT[...] = v.astype(BF)
        mixb[...] = dot(eye(TOK), mixT[...], NT).astype(BF)
        store(mixb, mix_o)

    def hgrad(p):
        routed = dot(GT[...], cotT[PAIR * p : PAIR * p + PAIR, :], NT).astype(BF)
        part = dot(routed, w[:, PAIR * p : PAIR * p + PAIR], NT)
        if p == 0:
            acc[...] = part
        elif p < 3:
            acc[...] += part
        else:
            hgb[...] = (acc[...] + part).astype(BF)
            store(hgb, hg_o)

    x1(0)
    ag(1, 0)
    mixed(0)
    ag(1, 1)
    x1b(0)
    x1(1)
    ag(2, 0)
    mixed(1)
    x2(0)
    ag(2, 1)
    x1(2)
    x2b(0)
    ag(3, 0)
    mixed(2)
    ag(3, 1)
    x3(0)
    x1(3)
    x1b(1)
    mixed(3)
    ag_last()
    rz(1)
    x1(4)
    rz(2)
    x2(1)
    x1b(2)
    rz(3)
    hgrad(0)
    x2b(1)
    rz(4)
    x2(2)
    hgrad(1)
    x1b(3)
    x3(1)
    rz_last()
    x2b(2)
    hgrad(2)
    x2(3)
    x1b(4)
    x3(2)
    hgrad(3)
    x2b(3)
    x2(4)
    x3(3)
    x2b(4)
    x3(4)

    lane = lax.broadcasted_iota(jnp.int32, (64, 128), 1)
    for p in range(4):
        a, b = OZ[2 * p], pltpu.roll(OZ[2 * p + 1], 64, 1)
        o = PAIR * p
        wgb[:, o : o + 384] = a[:, 0:384]
        wgb[:, o + 384 : o + 512] = jnp.where(lane < 64, a[:, 384:512], b[:, 0:128])
        wgb[:, o + 512 : o + 896] = b[:, 128:512]
    store(wgb, wg_o)
    for cp in stores:
        cp.wait()
    for cp in copies.values():
        cp.wait_send()


def body(hidden, down_weight, cotangent, expert_ids, gate_weights, row_token, tile_count):
    v = pltpu.VMEM
    scratch = [
        v((ROWS, HID), BF),
        v((HID, ROWS), BF),
        v((HID, ROWS), BF),
        v((HID, DIM), BF),
        v((TOK, BLK), BF),
        v((TOK, 8), jnp.int32),
        v((TOK, 8), BF),
        v((1, ROWS), jnp.int32),
        v((ROWS, TOK), BF),
        v((DIM, TOK), BF),
        v((ROWS, PAIR), BF),
    ]
    scratch += [v((4, 256, n), BF) for n in WIDTHS]
    scratch += [v((2, 128, n), BF) for n in WIDTHS]
    scratch += [v((2, 256, n), BF) for n in WIDTHS]
    scratch += [v((4, 64, n), BF) for n in WIDTHS]
    scratch += [v((2, 32, n), BF) for n in WIDTHS]
    scratch += [v((2, 64, n), BF) for n in WIDTHS]
    scratch += [v((64, n), F32) for n in WIDTHS]
    scratch += [
        v((NZ, 64, 512), F32),
        v((64, DIM), F32),
        v((2, NZ, BLK, TOK), BF),
        v((NZ, BLK, TOK), BF),
        v((2, 4, BLK, TOK), BF),
        v((2, 4, BLK, TOK), BF),
        v((ROWS, HID), F32),
        v((ROWS, HID), BF),
        v((TOK, BLK), BF),
        v((BLK, TOK), BF),
        pltpu.SemaphoreType.DMA((N_COPIES,)),
        pltpu.SemaphoreType.DMA((N_COPIES,)),
        pltpu.SemaphoreType.DMA((16,)),
    ]
    hbm = pl.BlockSpec(memory_space=pl.ANY)
    mixed_out, hidden_grad, weight_grad = pl.pallas_call(
        kernel,
        out_shape=(
            jax.ShapeDtypeStruct((TOK, BLK), BF),
            jax.ShapeDtypeStruct((ROWS, HID), BF),
            jax.ShapeDtypeStruct((64, DIM), F32),
        ),
        in_specs=[hbm] * 6 + [pl.BlockSpec(memory_space=pltpu.SMEM)],
        out_specs=(hbm, hbm, hbm),
        scratch_shapes=scratch,
        compiler_params=pltpu.CompilerParams(
            collective_id=0, has_side_effects=True, vmem_limit_bytes=64_000_000
        ),
    )(
        hidden[0, 0],
        down_weight[0],
        cotangent,
        expert_ids,
        gate_weights,
        row_token[0],
        tile_count,
    )
    return mixed_out, hidden_grad[None, None], weight_grad[None]


def solution(mesh):
    placed = (
        P("dp", "expert", None, None),
        P("expert", None, None),
        P("dp", "expert"),
        P("dp", None),
        P("dp", None),
        P("dp", "expert", None),
        P("dp", "expert"),
    )
    return jax.shard_map(
        body,
        mesh=mesh,
        in_specs=placed,
        out_specs=(P("dp", "expert"), P("dp", "expert", None, None), P("expert", "dp", None)),
        check_vma=False,
    )
```

```python
import jax
import jax.numpy as jnp
from jax import lax
from jax.experimental import pallas as pl
from jax.experimental.pallas import tpu as pltpu
from jax.sharding import PartitionSpec as P

MESH = pl.DeviceIdType.MESH
ROWS, HID, DIM, TOK = 384, 1024, 3584, 512
NZ = 8
BLK, SUB, ZBL, PAIR = 224, 112, 448, 896
CHUNKS = (
    ((0, 0, 384),),
    ((0, 384, 64), (1, 0, 112), (1, 224, 112), (-1, 0, 112), (-1, 224, 112)),
    ((1, 112, 112), (1, 336, 112), (-1, 112, 112), (-1, 336, 48)),
    ((-1, 384, 64), (2, 0, 448), (-2, 0, 384)),
    ((-2, 384, 64), (3, 0, 448), (-3, 0, 384)),
    ((-3, 384, 64), (4, 0, 448)),
)
WIDTHS = tuple(sum(n for _, _, n in pieces) for pieces in CHUNKS)
NCH = len(CHUNKS)
NT = (((1,), (1,)), ((), ()))
NN = (((1,), (0,)), ((), ()))
TN = (((0,), (0,)), ((), ()))
BF, F32 = jnp.bfloat16, jnp.float32
N_COPIES = 160


def dot(a, b, dims):
    return lax.dot_general(a, b, dims, preferred_element_type=F32)


def eye(n):
    return (
        lax.broadcasted_iota(jnp.int32, (n, n), 0) == lax.broadcasted_iota(jnp.int32, (n, n), 1)
    ).astype(F32).astype(BF)


def kernel(*refs):
    (hid_h, w_h, cot_h, ids_h, gw_h, tok_h, cnt_s, mix_o, hg_o, wg_o) = refs[:10]
    it = iter(refs[10:])
    nxt = lambda: next(it)
    hid, hT, hP, w, ids, gw, tok, GT, cotT = (nxt() for _ in range(9))
    RT = [nxt() for _ in range(NCH)]
    PB = [nxt() for _ in range(NCH)]
    RF = [nxt() for _ in range(NCH)]
    RN = [nxt() for _ in range(NCH)]
    S2 = [nxt() for _ in range(NCH)]
    RF2 = [nxt() for _ in range(NCH)]
    RN2 = [nxt() for _ in range(NCH)]
    FB = [nxt() for _ in range(NCH)]
    M, MR, ZS, ZR, acc = (nxt() for _ in range(5))
    mixT, hgb, OZ = mix_o, hg_o, wg_o
    send_sem, recv_sem, loc_sem = (nxt() for _ in range(3))

    dpi, ei = lax.axis_index("dp"), lax.axis_index("expert")
    x, y, z, c = dpi // 4, dpi % 4, ei // 2, ei % 2
    m1 = (1 - c) * x + c * y
    m2 = (1 - c) * y + c * x

    def dpid(p1, p2):
        return (1 - c) * (p1 * 4 + p2) + c * (p2 * 4 + p1)

    def zz(s):
        return (z + s + NZ) % NZ

    n1p = (dpid((m1 + 1) % 4, m2), ei)
    n1m = (dpid((m1 + 3) % 4, m2), ei)
    n2p = (dpid(m1, (m2 + 1) % 4), ei)
    n2m = (dpid(m1, (m2 + 3) % 4), ei)
    zp = (dpi, zz(1) * 2 + c)
    zm = (dpi, zz(-1) * 2 + c)
    pt = (dpi, z * 2 + 1 - c)

    loads = {}

    def load(name, src, dst):
        cp = pltpu.make_async_copy(src, dst, loc_sem.at[len(loads)])
        cp.start()
        loads[name] = cp

    own_row = pl.multiple_of(z * ZBL + c * BLK, 16)
    load("cot", cot_h, cotT.at[pl.ds(own_row, BLK)])
    load("ids", ids_h, ids)
    load("gw", gw_h, gw)
    load("tok", tok_h, tok)
    load("hid", hid_h, hid)
    for p in range(4):
        load(f"w{p}", w_h.at[:, pl.ds(p * PAIR, PAIR)], w.at[:, pl.ds(p * PAIR, PAIR)])

    barrier = pltpu.get_barrier_semaphore()
    for dev in (n1p, n1m, n2p, n2m, zp, zm, pt):
        pl.semaphore_signal(barrier, inc=1, device_id=dev, device_id_type=MESH)

    copies = {}

    def send(key, src, dst, dev):
        k = len(copies)
        cp = pltpu.make_async_remote_copy(
            src_ref=src,
            dst_ref=dst,
            send_sem=send_sem.at[k],
            recv_sem=recv_sem.at[k],
            device_id=dev,
            device_id_type=MESH,
        )
        cp.start()
        copies[key] = cp

    def got(*key):
        copies[key].wait_recv()

    def crow(s, core, sub, n=SUB):
        return cotT.at[pl.ds(pl.multiple_of(zz(s) * ZBL + core * BLK + sub * SUB, 16), n)]

    loads["cot"].wait()
    pl.semaphore_wait(barrier, 7)
    send(("p", 0), crow(0, c, 0, BLK), crow(0, c, 0, BLK), pt)
    for sub in range(2):
        send(("u", 0, sub), crow(0, c, sub), crow(0, c, sub), zp)
        send(("d", 0, sub), crow(0, c, sub), crow(0, c, sub), zm)

    loads["ids"].wait()
    loads["gw"].wait()
    loads["tok"].wait()
    gate_row = jnp.sum(
        jnp.where(ids[...] == ei, gw[...].astype(F32), 0.0), axis=0, keepdims=True
    )
    it_t = lax.broadcasted_iota(jnp.int32, (TOK, ROWS), 0)
    it_r = lax.broadcasted_iota(jnp.int32, (TOK, ROWS), 1)
    live = (tok[...] == it_t) & (it_r < cnt_s[0, 0] * 128)
    hot = jnp.where(live, 1.0, 0.0).astype(BF)
    GT[...] = (dot(eye(ROWS), hot, NT) * gate_row).astype(BF)

    loads["hid"].wait()
    for j in range(4):
        hT[256 * j : 256 * j + 256, :] = dot(
            eye(256), hid[:, 256 * j : 256 * j + 256], NT
        ).astype(BF)
    for r1 in range(4):
        for r2 in range(4):
            row = pl.multiple_of(64 * dpid((m1 + r1) % 4, (m2 + r2) % 4), 64)
            o = (r1 * 4 + r2) * 64
            hP[o : o + 64, :] = hT[pl.ds(row, 64), :]

    def ag(s, sub, dirn):
        got("ud"[dirn], s - 1, sub)
        src = crow(s if dirn else -s, c, sub)
        if s <= 2 or (s == 3 and sub == dirn):
            send(("ud"[dirn], s, sub), src, src, zm if dirn else zp)
        send(("p" + "ud"[dirn], s, sub), src, src, pt)

    def agl(dirn):
        got("ud"[dirn], 3, dirn)
        src = crow(4, c, dirn)
        send(("p" + "ud"[dirn], 4, dirn), src, src, pt)

    def x1a(k):
        if k == 0:
            got("p", 0)
        elif k == 5:
            got("pu", 4, 0)
            got("pd", 4, 1)
        else:
            for sub in {1: (0,), 2: (1,)}.get(k, (0, 1)):
                got("pu", max(k - 1, 1), sub)
                got("pd", max(k - 1, 1), sub)
        rows = [
            cotT[pl.ds(pl.multiple_of(zz(s) * ZBL + a, 16), n), :] for s, a, n in CHUNKS[k]
        ]
        rows = rows[0] if len(rows) == 1 else jnp.concatenate(rows, axis=0)
        RT[k][...] = dot(GT[...], rows, NT).astype(BF)
        pb, rf, rn = PB[k], RF[k], RN[k]
        for r1 in (2, 1, 3):
            pb[r1] = dot(hP[256 * r1 : 256 * r1 + 256, :], RT[k][...], NN).astype(BF)
            if r1 == 2:
                send(("F+", k), pb.at[2, pl.ds(0, 128)], rf.at[0], n1p)
                send(("F-", k), pb.at[2, pl.ds(128, 128)], rf.at[1], n1m)
            elif r1 == 1:
                send(("N+b", k), pb.at[1, pl.ds(128, 128)], rn.at[0, pl.ds(128, 128)], n1p)
            else:
                send(("N-a", k), pb.at[3, pl.ds(0, 128)], rn.at[1, pl.ds(0, 128)], n1m)

    def x1o(k):
        PB[k][0] = dot(hP[0:256, :], RT[k][...], NN).astype(BF)

    def x1b(k, dirn):
        pb, rf, rn = PB[k], RF[k], RN[k]
        if dirn == 0:
            got("F+", k)
            pb[1, 0:128, :] = (pb[1, 0:128, :].astype(F32) + rf[0].astype(F32)).astype(BF)
            send(("N+a", k), pb.at[1, pl.ds(0, 128)], rn.at[0, pl.ds(0, 128)], n1p)
        else:
            got("F-", k)
            pb[3, 128:256, :] = (pb[3, 128:256, :].astype(F32) + rf[1].astype(F32)).astype(BF)
            send(("N-b", k), pb.at[3, pl.ds(128, 128)], rn.at[1, pl.ds(128, 128)], n1m)

    def x2(k):
        pb, rn, s2, rf2, rn2 = PB[k], RN[k], S2[k], RF2[k], RN2[k]
        for key in ("N+b", "N-a", "N+a", "N-b"):
            got(key, k)
        for r2 in (2, 1, 3, 0):
            sl = slice(64 * r2, 64 * r2 + 64)
            tot = pb[0, sl, :].astype(F32) + rn[0, sl, :].astype(F32) + rn[1, sl, :].astype(F32)
            if r2 == 0:
                FB[k][...] = tot
            else:
                s2[r2] = tot.astype(BF)
            if r2 == 2:
                send(("f+", k), s2.at[2, pl.ds(0, 32)], rf2.at[0], n2p)
                send(("f-", k), s2.at[2, pl.ds(32, 32)], rf2.at[1], n2m)
            elif r2 == 1:
                send(("n+b", k), s2.at[1, pl.ds(32, 32)], rn2.at[0, pl.ds(32, 32)], n2p)
            elif r2 == 3:
                send(("n-a", k), s2.at[3, pl.ds(0, 32)], rn2.at[1, pl.ds(0, 32)], n2m)

    def x2b(k, dirn):
        s2, rf2, rn2 = S2[k], RF2[k], RN2[k]
        if dirn == 0:
            got("f+", k)
            s2[1, 0:32, :] = (s2[1, 0:32, :].astype(F32) + rf2[0].astype(F32)).astype(BF)
            send(("n+a", k), s2.at[1, pl.ds(0, 32)], rn2.at[0, pl.ds(0, 32)], n2p)
        else:
            got("f-", k)
            s2[3, 32:64, :] = (s2[3, 32:64, :].astype(F32) + rf2[1].astype(F32)).astype(BF)
            send(("n-b", k), s2.at[3, pl.ds(32, 32)], rn2.at[1, pl.ds(32, 32)], n2m)

    def x3(k):
        rn2 = RN2[k]
        for key in ("n+b", "n-a", "n+a", "n-b"):
            got(key, k)
        tot = FB[k][...] + rn2[0].astype(F32) + rn2[1].astype(F32)
        at = 0
        for s, a, n in CHUNKS[k]:
            OZ[zz(s), :, a : a + n] = tot[:, at : at + n]
            at += n

    def mixed(p):
        loads[f"w{p}"].wait()
        out = dot(hid[...], w[:, PAIR * p : PAIR * p + PAIR], NN).astype(BF)
        mt = dot(out, GT[...], TN).astype(BF)
        for k in range(2):
            for cc in range(2):
                o = ZBL * k + BLK * cc
                M[cc, 2 * p + k] = mt[o : o + BLK, :]
        send(("m", p), M.at[1 - c, pl.ds(2 * p, 2)], MR.at[pl.ds(2 * p, 2)], pt)

    def both(t, sl):
        return M[c, t, sl, :].astype(F32) + MR[t, sl, :].astype(F32)

    def rz(k, sub, dirn):
        if k == 1 and dirn == 0:
            for p in range(4):
                got("m", p)
        sl = slice(SUB * sub, SUB * sub + SUB)
        t = zz(k - 5) if dirn else zz(5 - k)
        v = both(t, sl)
        if k >= 3 or (k == 2 and sub == dirn):
            got("z", dirn, k - 1, sub)
            v = v + ZR[dirn, k - 2, sl, :].astype(F32)
        ZS[dirn, k - 1, sl, :] = v.astype(BF)
        send(
            ("z", dirn, k, sub),
            ZS.at[dirn, k - 1, pl.ds(SUB * sub, SUB)],
            ZR.at[dirn, k - 1, pl.ds(SUB * sub, SUB)],
            zm if dirn else zp,
        )

    def rzl():
        for sub in range(2):
            for dirn in range(2):
                got("z", dirn, 4, sub)
        v = both(z, slice(0, BLK)) + ZR[0, 3].astype(F32) + ZR[1, 3].astype(F32)
        mixT[...] = v.astype(BF)

    def hg(p):
        routed = dot(GT[...], cotT[PAIR * p : PAIR * p + PAIR, :], NT).astype(BF)
        part = dot(routed, w[:, PAIR * p : PAIR * p + PAIR], NT)
        if p == 0:
            acc[...] = part
        elif p < 3:
            acc[...] += part
        else:
            hgb[...] = (acc[...] + part).astype(BF)

    x1a(0)
    x1o(0)
    mixed(0)
    mixed(1)
    ag(1, 0, 0)
    ag(1, 0, 1)
    x1b(0, 0)
    x1b(0, 1)
    mixed(2)
    ag(1, 1, 0)
    ag(1, 1, 1)
    mixed(3)
    x2(0)
    x1a(1)
    x1a(2)
    ag(2, 0, 0)
    ag(2, 0, 1)
    rz(1, 0, 0)
    rz(1, 1, 1)
    rz(2, 0, 1)
    rz(2, 1, 0)
    x2b(0, 0)
    x2b(0, 1)
    x1o(1)
    x1o(2)
    ag(2, 1, 0)
    ag(2, 1, 1)
    x1b(1, 0)
    x1b(1, 1)
    x3(0)
    x1a(3)
    ag(3, 0, 0)
    ag(3, 0, 1)
    x1b(2, 0)
    x1b(2, 1)
    x1o(3)
    rz(2, 0, 0)
    rz(2, 1, 1)
    x2(1)
    rz(3, 1, 0)
    rz(3, 0, 1)
    x2b(1, 0)
    x2b(1, 1)
    x1b(3, 0)
    x1b(3, 1)
    ag(3, 1, 0)
    ag(3, 1, 1)
    x3(1)
    x1a(4)
    agl(0)
    x2(2)
    rz(3, 1, 1)
    x1o(4)
    rz(3, 0, 0)
    x2(3)
    rz(4, 0, 1)
    x2b(2, 0)
    x2b(2, 1)
    rz(4, 1, 0)
    agl(1)
    x2b(3, 0)
    x2b(3, 1)
    x1a(5)
    x1b(4, 0)
    x1b(4, 1)
    rz(4, 0, 0)
    rz(4, 1, 1)
    x1o(5)
    x3(2)
    hg(0)
    x3(3)
    hg(1)
    hg(2)
    x1b(5, 0)
    x1b(5, 1)
    hg(3)
    rzl()
    x2(4)
    x2(5)
    x2b(4, 0)
    x2b(4, 1)
    x2b(5, 0)
    x2b(5, 1)
    x3(4)
    x3(5)
    for cp in copies.values():
        cp.wait_send()


def finish(mix, hgr, blocks, mix_o, hg_o, wg_o, wgb, sem):
    first = pltpu.make_async_copy(hgr, hg_o, sem.at[4])
    second = pltpu.make_async_copy(mix, mix_o, sem.at[5])
    first.start()
    second.start()
    lane = lax.broadcasted_iota(jnp.int32, (64, 128), 1)
    rest = []
    for p in range(4):
        a, b = blocks[2 * p], pltpu.roll(blocks[2 * p + 1], 64, 1)
        o = PAIR * p
        wgb[:, o : o + 384] = a[:, 0:384]
        wgb[:, o + 384 : o + 512] = jnp.where(lane < 64, a[:, 384:512], b[:, 0:128])
        wgb[:, o + 512 : o + 896] = b[:, 128:512]
        cp = pltpu.make_async_copy(
            wgb.at[:, pl.ds(o, PAIR)], wg_o.at[:, pl.ds(o, PAIR)], sem.at[p]
        )
        cp.start()
        rest.append(cp)
    for cp in [first, second] + rest:
        cp.wait()


def body(hidden, down_weight, cotangent, expert_ids, gate_weights, row_token, tile_count):
    v = pltpu.VMEM
    scratch = [
        v((ROWS, HID), BF),
        v((HID, ROWS), BF),
        v((HID, ROWS), BF),
        v((HID, DIM), BF),
        v((8, TOK), jnp.int32),
        v((8, TOK), BF),
        v((1, ROWS), jnp.int32),
        v((ROWS, TOK), BF),
        v((DIM, TOK), BF),
    ]
    scratch += [v((ROWS, n), BF) for n in WIDTHS]
    scratch += [v((4, 256, n), BF) for n in WIDTHS]
    scratch += [v((2, 128, n), BF) for n in WIDTHS]
    scratch += [v((2, 256, n), BF) for n in WIDTHS]
    scratch += [v((4, 64, n), BF) for n in WIDTHS]
    scratch += [v((2, 32, n), BF) for n in WIDTHS]
    scratch += [v((2, 64, n), BF) for n in WIDTHS]
    scratch += [v((64, n), F32) for n in WIDTHS]
    scratch += [
        v((2, NZ, BLK, TOK), BF),
        v((NZ, BLK, TOK), BF),
        v((2, 4, BLK, TOK), BF),
        v((2, 4, BLK, TOK), BF),
        v((ROWS, HID), F32),
        pltpu.SemaphoreType.DMA((N_COPIES,)),
        pltpu.SemaphoreType.DMA((N_COPIES,)),
        pltpu.SemaphoreType.DMA((16,)),
    ]
    hbm = pl.BlockSpec(memory_space=pl.ANY)
    vm = pl.BlockSpec(memory_space=pltpu.VMEM)
    raw = pl.pallas_call(
        kernel,
        out_shape=(v((BLK, TOK), BF), v((ROWS, HID), BF), v((NZ, 64, 512), F32)),
        in_specs=[hbm] * 6 + [pl.BlockSpec(memory_space=pltpu.SMEM)],
        out_specs=(vm, vm, vm),
        scratch_shapes=scratch,
        compiler_params=pltpu.CompilerParams(
            collective_id=0, has_side_effects=True, vmem_limit_bytes=58_000_000
        ),
    )(
        hidden[0, 0],
        down_weight[0],
        cotangent.T,
        expert_ids.T,
        gate_weights.T,
        row_token[0],
        tile_count,
    )
    mixed_out, hidden_grad, weight_grad = pl.pallas_call(
        finish,
        out_shape=(
            jax.ShapeDtypeStruct((BLK, TOK), BF),
            jax.ShapeDtypeStruct((ROWS, HID), BF),
            jax.ShapeDtypeStruct((64, DIM), F32),
        ),
        in_specs=[vm] * 3,
        out_specs=(hbm,) * 3,
        scratch_shapes=[v((64, DIM), F32), pltpu.SemaphoreType.DMA((6,))],
        compiler_params=pltpu.CompilerParams(vmem_limit_bytes=4_000_000),
    )(*raw)
    return mixed_out.T, hidden_grad[None, None], weight_grad[None]


def solution(mesh):
    placed = (
        P("dp", "expert", None, None),
        P("expert", None, None),
        P("dp", "expert"),
        P("dp", None),
        P("dp", None),
        P("dp", "expert", None),
        P("dp", "expert"),
    )
    return jax.shard_map(
        body,
        mesh=mesh,
        in_specs=placed,
        out_specs=(P("dp", "expert"), P("dp", "expert", None, None), P("expert", "dp", None)),
        check_vma=False,
    )
```

```python
import jax
import jax.numpy as jnp
from jax import lax
from jax.experimental import pallas as pl
from jax.experimental.pallas import tpu as pltpu
from jax.sharding import PartitionSpec as P

MESH = pl.DeviceIdType.MESH
ROWS, HID, DIM, TOK = 384, 1024, 3584, 512
NZ = 8
BLK, SUB, ZBL, PAIR = 224, 112, 448, 896
CHUNKS = (
    ((0, 0, 384),),
    ((0, 384, 64), (1, 0, 80), (1, 224, 80), (-1, 0, 80), (-1, 224, 80)),
    ((1, 80, 144), (1, 304, 144), (-1, 80, 144), (-1, 304, 80)),
    ((-1, 384, 64), (2, 0, 448), (-2, 0, 384)),
    ((-2, 384, 64), (3, 0, 448), (-3, 0, 384)),
    ((-3, 384, 64), (4, 0, 320)),
    ((4, 320, 128),),
)
WIDTHS = tuple(sum(n for _, _, n in pieces) for pieces in CHUNKS)
NCH = len(CHUNKS)
END = NCH - 1
PIECE = (80, 144)
N_SEND, N_RECV = 48, 74
NT = (((1,), (1,)), ((), ()))
NN = (((1,), (0,)), ((), ()))
TN = (((0,), (0,)), ((), ()))
BF, F32 = jnp.bfloat16, jnp.float32


def dot(a, b, dims):
    return lax.dot_general(a, b, dims, preferred_element_type=F32)


def eye(n):
    return (
        lax.broadcasted_iota(jnp.int32, (n, n), 0) == lax.broadcasted_iota(jnp.int32, (n, n), 1)
    ).astype(F32).astype(BF)


def kernel(*refs):
    (hid_h, w_h, cot_h, ids_h, gw_h, tok_h, cnt_s, mix_o, hg_o, wg_o) = refs[:10]
    it = iter(refs[10:])
    nxt = lambda: next(it)
    hid, hT, hP, w, ids, gw, tok, GT, cotT = (nxt() for _ in range(9))
    RT = [nxt() for _ in range(NCH)]
    PB = [nxt() for _ in range(NCH)]
    RF = [nxt() for _ in range(NCH)]
    RN = [nxt() for _ in range(NCH)]
    S2 = [nxt() for _ in range(NCH)]
    RF2 = [nxt() for _ in range(NCH)]
    RN2 = [nxt() for _ in range(NCH)]
    FB = [nxt() for _ in range(NCH)]
    M, MR, ZS, ZR, acc = (nxt() for _ in range(5))
    mixT, hgb, OZ = mix_o, hg_o, wg_o
    send_sem, recv_sem, loc_sem = (nxt() for _ in range(3))

    dpi, ei = lax.axis_index("dp"), lax.axis_index("expert")
    x, y, z, c = dpi // 4, dpi % 4, ei // 2, ei % 2
    m1 = (1 - c) * x + c * y
    m2 = (1 - c) * y + c * x

    def dpid(p1, p2):
        return (1 - c) * (p1 * 4 + p2) + c * (p2 * 4 + p1)

    def zz(s):
        return (z + s + NZ) % NZ

    n1p = (dpid((m1 + 1) % 4, m2), ei)
    n1m = (dpid((m1 + 3) % 4, m2), ei)
    n2p = (dpid(m1, (m2 + 1) % 4), ei)
    n2m = (dpid(m1, (m2 + 3) % 4), ei)
    n2f = (dpid(m1, (m2 + 2) % 4), ei)
    zp = (dpi, zz(1) * 2 + c)
    zm = (dpi, zz(-1) * 2 + c)
    pt = (dpi, z * 2 + 1 - c)

    loads = {}

    def load(name, src, dst):
        cp = pltpu.make_async_copy(src, dst, loc_sem.at[len(loads)])
        cp.start()
        loads[name] = cp

    own_row = pl.multiple_of(z * ZBL + c * BLK, 16)
    load("cot", cot_h, cotT.at[pl.ds(own_row, BLK)])
    load("ids", ids_h, ids)
    load("gw", gw_h, gw)
    load("tok", tok_h, tok)
    load("hid", hid_h, hid)
    for p in range(4):
        load(f"w{p}", w_h.at[:, pl.ds(p * PAIR, PAIR)], w.at[:, pl.ds(p * PAIR, PAIR)])

    barrier = pltpu.get_barrier_semaphore()
    for dev in (n1p, n1m, n2p, n2m, n2f, zp, zm, pt):
        pl.semaphore_signal(barrier, inc=1, device_id=dev, device_id_type=MESH)

    slots, waited, sent = {}, set(), []

    def group(key):
        name, rest = key[0], key[1:]
        if name in ("pu", "pd"):
            return ("P",) + (rest if rest[0] == 1 else rest[:1])
        if name == "m":
            return ("m",)
        if name == "z" and rest[1] == 4:
            return ("Z", rest[0])
        if name[0] in "Nn":
            return (name[0], rest[0])
        return key

    def remote(src, dst, k, q, dev):
        return pltpu.make_async_remote_copy(
            src_ref=src,
            dst_ref=dst,
            send_sem=send_sem.at[k],
            recv_sem=recv_sem.at[q],
            device_id=dev,
            device_id_type=MESH,
        )

    def send(key, src, dst, dev):
        q = slots.setdefault(group(key), len(slots))
        k = len(sent)
        if k >= N_SEND:
            sent[k - N_SEND].wait_send()
        cp = remote(src, dst, k % N_SEND, q, dev)
        cp.start()
        sent.append(cp)

    def take(key, whole):
        if key not in waited:
            waited.add(key)
            remote(whole, whole, 0, slots[key], pt).wait_recv()

    def crow(s, core, sub):
        at = pl.multiple_of(zz(s) * ZBL + core * BLK + sub * PIECE[0], 16)
        return cotT.at[pl.ds(at, PIECE[sub])]

    def span(n):
        return cotT.at[pl.ds(0, n)]

    loads["cot"].wait()
    pl.semaphore_wait(barrier, 8)
    own = cotT.at[pl.ds(own_row, BLK)]
    send(("p", 0), own, own, pt)
    for sub in range(2):
        send(("u", 0, sub), crow(0, c, sub), crow(0, c, sub), zp)
        send(("d", 0, sub), crow(0, c, sub), crow(0, c, sub), zm)

    loads["ids"].wait()
    loads["gw"].wait()
    loads["tok"].wait()
    gate_row = jnp.sum(
        jnp.where(ids[...] == ei, gw[...].astype(F32), 0.0), axis=0, keepdims=True
    )
    it_t = lax.broadcasted_iota(jnp.int32, (TOK, ROWS), 0)
    it_r = lax.broadcasted_iota(jnp.int32, (TOK, ROWS), 1)
    live = (tok[...] == it_t) & (it_r < cnt_s[0, 0] * 128)
    hot = jnp.where(live, 1.0, 0.0).astype(BF)
    GT[...] = (dot(eye(ROWS), hot, NT) * gate_row).astype(BF)

    loads["hid"].wait()
    for j in range(4):
        hT[256 * j : 256 * j + 256, :] = dot(
            eye(256), hid[:, 256 * j : 256 * j + 256], NT
        ).astype(BF)
    for r1 in range(4):
        for r2 in range(4):
            row = pl.multiple_of(64 * dpid((m1 + r1) % 4, (m2 + r2) % 4), 64)
            o = (r1 * 4 + r2) * 64
            hP[o : o + 64, :] = hT[pl.ds(row, 64), :]

    def ag(s, sub, dirn):
        take(("ud"[dirn], s - 1, sub), span(PIECE[sub]))
        src = crow(s if dirn else -s, c, sub)
        if s <= 2 or (s == 3 and sub == dirn):
            send(("ud"[dirn], s, sub), src, src, zm if dirn else zp)
        send(("p" + "ud"[dirn], s, sub), src, src, pt)

    def agl(dirn):
        take(("ud"[dirn], 3, dirn), span(PIECE[dirn]))
        src = crow(4, c, dirn)
        send(("p" + "ud"[dirn], 4, dirn), src, src, pt)

    def x1a(k):
        if k == 0:
            take(("p", 0), span(BLK))
        elif k <= 2:
            take(("P", 1, k - 1), span(2 * PIECE[k - 1]))
        elif k < END:
            take(("P", k - 1), span(BLK if k == 5 else 2 * BLK))
        rows = [
            cotT[pl.ds(pl.multiple_of(zz(s) * ZBL + a, 16), n), :] for s, a, n in CHUNKS[k]
        ]
        rows = rows[0] if len(rows) == 1 else jnp.concatenate(rows, axis=0)
        RT[k][...] = dot(GT[...], rows, NT).astype(BF)
        pb, rf, rn = PB[k], RF[k], RN[k]
        for r1 in (2, 1, 3):
            pb[r1] = dot(hP[256 * r1 : 256 * r1 + 256, :], RT[k][...], NN).astype(BF)
            if r1 == 2:
                send(("F+", k), pb.at[2, pl.ds(0, 128)], rf.at[0], n1p)
                send(("F-", k), pb.at[2, pl.ds(128, 128)], rf.at[1], n1m)
            elif r1 == 1:
                send(("N+b", k), pb.at[1, pl.ds(128, 128)], rn.at[0, pl.ds(128, 128)], n1p)
            else:
                send(("N-a", k), pb.at[3, pl.ds(0, 128)], rn.at[1, pl.ds(0, 128)], n1m)

    def x1o(k):
        PB[k][0] = dot(hP[0:256, :], RT[k][...], NN).astype(BF)

    def x1b(k, dirn):
        pb, rf, rn = PB[k], RF[k], RN[k]
        if dirn == 0:
            take(("F+", k), rf.at[0])
            pb[1, 0:128, :] = (pb[1, 0:128, :].astype(F32) + rf[0].astype(F32)).astype(BF)
            send(("N+a", k), pb.at[1, pl.ds(0, 128)], rn.at[0, pl.ds(0, 128)], n1p)
        else:
            take(("F-", k), rf.at[1])
            pb[3, 128:256, :] = (pb[3, 128:256, :].astype(F32) + rf[1].astype(F32)).astype(BF)
            send(("N-b", k), pb.at[3, pl.ds(128, 128)], rn.at[1, pl.ds(128, 128)], n1m)

    def x2(k):
        pb, rn, s2, rf2, rn2 = PB[k], RN[k], S2[k], RF2[k], RN2[k]
        take(("N", k), rn)
        for r2 in (2, 1, 3, 0):
            sl = slice(64 * r2, 64 * r2 + 64)
            tot = pb[0, sl, :].astype(F32) + rn[0, sl, :].astype(F32) + rn[1, sl, :].astype(F32)
            if r2 == 0:
                FB[k][...] = tot
            else:
                s2[r2] = tot.astype(BF)
            if k == END:
                if r2:
                    to = (rn2.at[0], rf2, rn2.at[1])[r2 - 1]
                    dev = (n2p, n2f, n2m)[r2 - 1]
                    send((("n+", "ff", "n-")[r2 - 1], k), s2.at[r2], to, dev)
            elif r2 == 2:
                send(("f+", k), s2.at[2, pl.ds(0, 32)], rf2.at[0], n2p)
                send(("f-", k), s2.at[2, pl.ds(32, 32)], rf2.at[1], n2m)
            elif r2 == 1:
                send(("n+b", k), s2.at[1, pl.ds(32, 32)], rn2.at[0, pl.ds(32, 32)], n2p)
            elif r2 == 3:
                send(("n-a", k), s2.at[3, pl.ds(0, 32)], rn2.at[1, pl.ds(0, 32)], n2m)

    def x2b(k, dirn):
        s2, rf2, rn2 = S2[k], RF2[k], RN2[k]
        if dirn == 0:
            take(("f+", k), rf2.at[0])
            s2[1, 0:32, :] = (s2[1, 0:32, :].astype(F32) + rf2[0].astype(F32)).astype(BF)
            send(("n+a", k), s2.at[1, pl.ds(0, 32)], rn2.at[0, pl.ds(0, 32)], n2p)
        else:
            take(("f-", k), rf2.at[1])
            s2[3, 32:64, :] = (s2[3, 32:64, :].astype(F32) + rf2[1].astype(F32)).astype(BF)
            send(("n-b", k), s2.at[3, pl.ds(32, 32)], rn2.at[1, pl.ds(32, 32)], n2m)

    def x3(k):
        rn2 = RN2[k]
        take(("n", k), rn2)
        tot = FB[k][...] + rn2[0].astype(F32) + rn2[1].astype(F32)
        if k == END:
            take(("ff", k), RF2[k])
            tot = tot + RF2[k][...].astype(F32)
        at = 0
        for s, a, n in CHUNKS[k]:
            OZ[zz(s), :, a : a + n] = tot[:, at : at + n]
            at += n

    def mixed(p):
        loads[f"w{p}"].wait()
        out = dot(hid[...], w[:, PAIR * p : PAIR * p + PAIR], NN).astype(BF)
        mt = dot(out, GT[...], TN).astype(BF)
        for k in range(2):
            for cc in range(2):
                o = ZBL * k + BLK * cc
                M[cc, 2 * p + k] = mt[o : o + BLK, :]
        send(("m", p), M.at[1 - c, pl.ds(2 * p, 2)], MR.at[pl.ds(2 * p, 2)], pt)

    def both(t, sl):
        return M[c, t, sl, :].astype(F32) + MR[t, sl, :].astype(F32)

    def rz(k, sub, dirn):
        take(("m",), MR)
        sl = slice(SUB * sub, SUB * sub + SUB)
        t = zz(k - 5) if dirn else zz(5 - k)
        v = both(t, sl)
        if k >= 3 or (k == 2 and sub == dirn):
            take(("z", dirn, k - 1, sub), ZR.at[dirn, k - 2, pl.ds(SUB * sub, SUB)])
            v = v + ZR[dirn, k - 2, sl, :].astype(F32)
        ZS[dirn, k - 1, sl, :] = v.astype(BF)
        send(
            ("z", dirn, k, sub),
            ZS.at[dirn, k - 1, pl.ds(SUB * sub, SUB)],
            ZR.at[dirn, k - 1, pl.ds(SUB * sub, SUB)],
            zm if dirn else zp,
        )

    def rzl():
        for dirn in range(2):
            take(("Z", dirn), ZR.at[dirn, 3])
        v = both(z, slice(0, BLK)) + ZR[0, 3].astype(F32) + ZR[1, 3].astype(F32)
        mixT[...] = v.astype(BF)

    def hg(p):
        routed = dot(GT[...], cotT[PAIR * p : PAIR * p + PAIR, :], NT).astype(BF)
        part = dot(routed, w[:, PAIR * p : PAIR * p + PAIR], NT)
        if p == 0:
            acc[...] = part
        elif p < 3:
            acc[...] += part
        else:
            hgb[...] = (acc[...] + part).astype(BF)

    x1a(0)
    x1o(0)
    ag(1, 0, 0)
    ag(1, 0, 1)
    x1b(0, 0)
    x1b(0, 1)
    x1a(1)
    ag(1, 1, 1)
    ag(1, 1, 0)
    mixed(0)
    x2(0)
    ag(2, 0, 0)
    x1a(2)
    x1b(1, 1)
    x1b(1, 0)
    ag(2, 0, 1)
    mixed(1)
    x2b(0, 1)
    x2b(0, 0)
    x1o(2)
    x1o(1)
    ag(2, 1, 1)
    ag(2, 1, 0)
    x1b(2, 1)
    x1b(2, 0)
    x1a(3)
    ag(3, 0, 0)
    x3(0)
    x2(1)
    ag(3, 0, 1)
    mixed(2)
    x2(2)
    ag(3, 1, 1)
    ag(3, 1, 0)
    mixed(3)
    x2b(1, 0)
    x2b(1, 1)
    x2b(2, 1)
    x1b(3, 1)
    x2b(2, 0)
    x1b(3, 0)
    agl(0)
    rz(1, 0, 0)
    rz(1, 1, 1)
    x1a(4)
    agl(1)
    rz(2, 0, 1)
    rz(2, 1, 0)
    x3(1)
    x3(2)
    x1a(5)
    rz(2, 0, 0)
    x1a(6)
    rz(2, 1, 1)
    hg(0)
    rz(3, 1, 0)
    rz(3, 0, 1)
    x1o(5)
    x1b(4, 0)
    x1b(4, 1)
    hg(1)
    rz(3, 0, 0)
    hg(2)
    x1o(6)
    x1b(5, 0)
    rz(3, 1, 1)
    x1b(5, 1)
    x1o(3)
    x1o(4)
    x1b(6, 1)
    x1b(6, 0)
    rz(4, 1, 0)
    rz(4, 0, 1)
    hg(3)
    rz(4, 0, 0)
    x2(3)
    x2(4)
    rz(4, 1, 1)
    x2(5)
    x2b(3, 1)
    x2(6)
    x2b(3, 0)
    x2b(4, 0)
    x2b(4, 1)
    x2b(5, 0)
    x2b(5, 1)
    x3(6)
    x3(3)
    x3(4)
    rzl()
    x3(5)
    assert len(slots) == N_RECV
    for cp in sent[-N_SEND:]:
        cp.wait_send()


def finish(mix, hgr, blocks, mix_o, hg_o, wg_o, wgb, sem):
    first = pltpu.make_async_copy(hgr, hg_o, sem.at[4])
    second = pltpu.make_async_copy(mix, mix_o, sem.at[5])
    first.start()
    second.start()
    lane = lax.broadcasted_iota(jnp.int32, (64, 128), 1)
    rest = []
    for p in range(4):
        a, b = blocks[2 * p], pltpu.roll(blocks[2 * p + 1], 64, 1)
        o = PAIR * p
        wgb[:, o : o + 384] = a[:, 0:384]
        wgb[:, o + 384 : o + 512] = jnp.where(lane < 64, a[:, 384:512], b[:, 0:128])
        wgb[:, o + 512 : o + 896] = b[:, 128:512]
        cp = pltpu.make_async_copy(
            wgb.at[:, pl.ds(o, PAIR)], wg_o.at[:, pl.ds(o, PAIR)], sem.at[p]
        )
        cp.start()
        rest.append(cp)
    for cp in [first, second] + rest:
        cp.wait()


def body(hidden, down_weight, cotangent, expert_ids, gate_weights, row_token, tile_count):
    v = pltpu.VMEM
    scratch = [
        v((ROWS, HID), BF),
        v((HID, ROWS), BF),
        v((HID, ROWS), BF),
        v((HID, DIM), BF),
        v((8, TOK), jnp.int32),
        v((8, TOK), BF),
        v((1, ROWS), jnp.int32),
        v((ROWS, TOK), BF),
        v((DIM, TOK), BF),
    ]
    scratch += [v((ROWS, n), BF) for n in WIDTHS]
    scratch += [v((4, 256, n), BF) for n in WIDTHS]
    scratch += [v((2, 128, n), BF) for n in WIDTHS]
    scratch += [v((2, 256, n), BF) for n in WIDTHS]
    scratch += [v((4, 64, n), BF) for n in WIDTHS]
    scratch += [v((2, 32, n), BF) for n in WIDTHS[:-1]] + [v((64, WIDTHS[-1]), BF)]
    scratch += [v((2, 64, n), BF) for n in WIDTHS]
    scratch += [v((64, n), F32) for n in WIDTHS]
    scratch += [
        v((2, NZ, BLK, TOK), BF),
        v((NZ, BLK, TOK), BF),
        v((2, 4, BLK, TOK), BF),
        v((2, 4, BLK, TOK), BF),
        v((ROWS, HID), F32),
        pltpu.SemaphoreType.DMA((N_SEND,)),
        pltpu.SemaphoreType.DMA((N_RECV,)),
        pltpu.SemaphoreType.DMA((9,)),
    ]
    hbm = pl.BlockSpec(memory_space=pl.ANY)
    vm = pl.BlockSpec(memory_space=pltpu.VMEM)
    raw = pl.pallas_call(
        kernel,
        out_shape=(v((BLK, TOK), BF), v((ROWS, HID), BF), v((NZ, 64, 512), F32)),
        in_specs=[hbm] * 6 + [pl.BlockSpec(memory_space=pltpu.SMEM)],
        out_specs=(vm, vm, vm),
        scratch_shapes=scratch,
        compiler_params=pltpu.CompilerParams(
            collective_id=0, has_side_effects=True, vmem_limit_bytes=58_000_000
        ),
    )(
        hidden[0, 0],
        down_weight[0],
        cotangent.T,
        expert_ids.T,
        gate_weights.T,
        row_token[0],
        tile_count,
    )
    mixed_out, hidden_grad, weight_grad = pl.pallas_call(
        finish,
        out_shape=(
            jax.ShapeDtypeStruct((BLK, TOK), BF),
            jax.ShapeDtypeStruct((ROWS, HID), BF),
            jax.ShapeDtypeStruct((64, DIM), F32),
        ),
        in_specs=[vm] * 3,
        out_specs=(hbm,) * 3,
        scratch_shapes=[v((64, DIM), F32), pltpu.SemaphoreType.DMA((6,))],
        compiler_params=pltpu.CompilerParams(vmem_limit_bytes=4_000_000),
    )(*raw)
    return mixed_out.T, hidden_grad[None, None], weight_grad[None]


def solution(mesh):
    placed = (
        P("dp", "expert", None, None),
        P("expert", None, None),
        P("dp", "expert"),
        P("dp", None),
        P("dp", None),
        P("dp", "expert", None),
        P("dp", "expert"),
    )
    return jax.shard_map(
        body,
        mesh=mesh,
        in_specs=placed,
        out_specs=(P("dp", "expert"), P("dp", "expert", None, None), P("expert", "dp", None)),
        check_vma=False,
    )
```

```python
import jax
import jax.numpy as jnp
from jax import lax
from jax.experimental import pallas as pl
from jax.experimental.pallas import tpu as pltpu
from jax.sharding import PartitionSpec as P

MESH = pl.DeviceIdType.MESH
ROWS, HID, DIM, TOK = 384, 1024, 3584, 512
NZ = 8
BLK, SUB, ZBL, PAIR = 224, 112, 448, 896
CHUNKS = (
    ((0, 0, 384),),
    ((0, 384, 64), (1, 0, 80), (1, 224, 80), (-1, 0, 80), (-1, 224, 80)),
    ((1, 80, 144), (1, 304, 144), (-1, 80, 144), (-1, 304, 80)),
    ((-1, 384, 64), (2, 0, 448), (-2, 0, 384)),
    ((-2, 384, 64), (3, 0, 448), (-3, 0, 384)),
    ((-3, 384, 64), (4, 0, 320)),
    ((4, 320, 128),),
)
WIDTHS = tuple(sum(n for _, _, n in pieces) for pieces in CHUNKS)
NCH = len(CHUNKS)
END = NCH - 1
PIECE = (80, 144)
N_SEND, N_RECV = 32, 74
NT = (((1,), (1,)), ((), ()))
NN = (((1,), (0,)), ((), ()))
TN = (((0,), (0,)), ((), ()))
BF, F32 = jnp.bfloat16, jnp.float32


def dot(a, b, dims):
    return lax.dot_general(a, b, dims, preferred_element_type=F32)


def eye(n):
    return (
        lax.broadcasted_iota(jnp.int32, (n, n), 0) == lax.broadcasted_iota(jnp.int32, (n, n), 1)
    ).astype(F32).astype(BF)


def kernel(*refs):
    (hid_h, w_h, cot_h, ids_h, gw_h, tok_h, cnt_s, mix_o, hg_o, wg_o) = refs[:10]
    it = iter(refs[10:])
    nxt = lambda: next(it)
    hid, hT, hP, w, ids, gw, tok, GT, cotT = (nxt() for _ in range(9))
    RT = [nxt() for _ in range(NCH)]
    PB = [nxt() for _ in range(NCH)]
    RF = [nxt() for _ in range(NCH)]
    RN = [nxt() for _ in range(NCH)]
    S2 = [nxt() for _ in range(NCH)]
    RF2 = [nxt() for _ in range(NCH)]
    RN2 = [nxt() for _ in range(NCH)]
    FB = [nxt() for _ in range(NCH)]
    M, MR, ZS, ZR, acc = (nxt() for _ in range(5))
    mixT, hgb, OZ = mix_o, hg_o, wg_o
    send_sem, recv_sem, loc_sem = (nxt() for _ in range(3))

    dpi, ei = lax.axis_index("dp"), lax.axis_index("expert")
    x, y, z, c = dpi // 4, dpi % 4, ei // 2, ei % 2
    m1 = (1 - c) * x + c * y
    m2 = (1 - c) * y + c * x

    def dpid(p1, p2):
        return (1 - c) * (p1 * 4 + p2) + c * (p2 * 4 + p1)

    def zz(s):
        return (z + s + NZ) % NZ

    n1p = (dpid((m1 + 1) % 4, m2), ei)
    n1m = (dpid((m1 + 3) % 4, m2), ei)
    n2p = (dpid(m1, (m2 + 1) % 4), ei)
    n2m = (dpid(m1, (m2 + 3) % 4), ei)
    n2f = (dpid(m1, (m2 + 2) % 4), ei)
    zp = (dpi, zz(1) * 2 + c)
    zm = (dpi, zz(-1) * 2 + c)
    pt = (dpi, z * 2 + 1 - c)

    barrier = pltpu.get_barrier_semaphore()
    for dev in (n1p, n1m, n2p, n2m, n2f, zp, zm, pt):
        pl.semaphore_signal(barrier, inc=1, device_id=dev, device_id_type=MESH)

    loads = {}

    def load(name, src, dst):
        cp = pltpu.make_async_copy(src, dst, loc_sem.at[len(loads)])
        cp.start()
        loads[name] = cp

    own_row = pl.multiple_of(z * ZBL + c * BLK, 16)
    load("cot", cot_h, cotT.at[pl.ds(own_row, BLK)])
    load("ids", ids_h, ids)
    load("gw", gw_h, gw)
    load("tok", tok_h, tok)
    load("hid", hid_h, hid)

    slots, waited, sent = {}, set(), []

    def group(key):
        name, rest = key[0], key[1:]
        if name in ("pu", "pd"):
            return ("P",) + (rest if rest[0] == 1 else rest[:1])
        if name == "m":
            return ("m",)
        if name == "z" and rest[1] == 4:
            return ("Z", rest[0])
        if name[0] in "Nn":
            return (name[0], rest[0])
        return key

    def remote(src, dst, k, q, dev):
        return pltpu.make_async_remote_copy(
            src_ref=src,
            dst_ref=dst,
            send_sem=send_sem.at[k],
            recv_sem=recv_sem.at[q],
            device_id=dev,
            device_id_type=MESH,
        )

    def send(key, src, dst, dev):
        q = slots.setdefault(group(key), len(slots))
        k = len(sent)
        if k >= N_SEND:
            sent[k - N_SEND].wait_send()
        cp = remote(src, dst, k % N_SEND, q, dev)
        cp.start()
        sent.append(cp)

    def take(key, whole):
        if key not in waited:
            waited.add(key)
            remote(whole, whole, 0, slots[key], pt).wait_recv()

    def crow(s, core, sub):
        at = pl.multiple_of(zz(s) * ZBL + core * BLK + sub * PIECE[0], 16)
        return cotT.at[pl.ds(at, PIECE[sub])]

    def span(n):
        return cotT.at[pl.ds(0, n)]

    pl.semaphore_wait(barrier, 8)
    for sub in range(2):
        piece = cot_h.at[pl.ds(PIECE[0] * sub, PIECE[sub])]
        send(("u", 0, sub), piece, crow(0, c, sub), zp)
        send(("d", 0, sub), piece, crow(0, c, sub), zm)
        if sub == 0:
            send(("p", 0), cot_h, cotT.at[pl.ds(own_row, BLK)], pt)

    for p in range(4):
        load(f"w{p}", w_h.at[:, pl.ds(p * PAIR, PAIR)], w.at[:, pl.ds(p * PAIR, PAIR)])

    loads["cot"].wait()
    loads["ids"].wait()
    loads["gw"].wait()
    loads["tok"].wait()
    gate_row = jnp.sum(
        jnp.where(ids[...] == ei, gw[...].astype(F32), 0.0), axis=0, keepdims=True
    )
    it_t = lax.broadcasted_iota(jnp.int32, (TOK, ROWS), 0)
    it_r = lax.broadcasted_iota(jnp.int32, (TOK, ROWS), 1)
    live = (tok[...] == it_t) & (it_r < cnt_s[0, 0] * 128)
    hot = jnp.where(live, 1.0, 0.0).astype(BF)
    GT[...] = (dot(eye(ROWS), hot, NT) * gate_row).astype(BF)

    loads["hid"].wait()
    for j in range(4):
        hT[256 * j : 256 * j + 256, :] = dot(
            eye(256), hid[:, 256 * j : 256 * j + 256], NT
        ).astype(BF)
    for r1 in range(4):
        for r2 in range(4):
            row = pl.multiple_of(64 * dpid((m1 + r1) % 4, (m2 + r2) % 4), 64)
            o = (r1 * 4 + r2) * 64
            hP[o : o + 64, :] = hT[pl.ds(row, 64), :]

    def ag(s, sub, dirn):
        take(("ud"[dirn], s - 1, sub), span(PIECE[sub]))
        src = crow(s if dirn else -s, c, sub)
        if s <= 2 or (s == 3 and sub == dirn):
            send(("ud"[dirn], s, sub), src, src, zm if dirn else zp)
        send(("p" + "ud"[dirn], s, sub), src, src, pt)

    def agl(dirn):
        take(("ud"[dirn], 3, dirn), span(PIECE[dirn]))
        src = crow(4, c, dirn)
        send(("p" + "ud"[dirn], 4, dirn), src, src, pt)

    def x1a(k):
        if k == 0:
            take(("p", 0), span(BLK))
        elif k <= 2:
            take(("P", 1, k - 1), span(2 * PIECE[k - 1]))
        elif k < END:
            take(("P", k - 1), span(BLK if k == 5 else 2 * BLK))
        rows = [
            cotT[pl.ds(pl.multiple_of(zz(s) * ZBL + a, 16), n), :] for s, a, n in CHUNKS[k]
        ]
        rows = rows[0] if len(rows) == 1 else jnp.concatenate(rows, axis=0)
        RT[k][...] = dot(GT[...], rows, NT).astype(BF)
        pb, rf, rn = PB[k], RF[k], RN[k]
        for r1 in (2, 1, 3):
            pb[r1] = dot(hP[256 * r1 : 256 * r1 + 256, :], RT[k][...], NN).astype(BF)
            if r1 == 2:
                send(("F+", k), pb.at[2, pl.ds(0, 128)], rf.at[0], n1p)
                send(("F-", k), pb.at[2, pl.ds(128, 128)], rf.at[1], n1m)
            elif r1 == 1:
                send(("N+b", k), pb.at[1, pl.ds(128, 128)], rn.at[0, pl.ds(128, 128)], n1p)
            else:
                send(("N-a", k), pb.at[3, pl.ds(0, 128)], rn.at[1, pl.ds(0, 128)], n1m)

    def x1o(k):
        PB[k][0] = dot(hP[0:256, :], RT[k][...], NN).astype(BF)

    def x1b(k, dirn):
        pb, rf, rn = PB[k], RF[k], RN[k]
        if dirn == 0:
            take(("F+", k), rf.at[0])
            pb[1, 0:128, :] = (pb[1, 0:128, :].astype(F32) + rf[0].astype(F32)).astype(BF)
            send(("N+a", k), pb.at[1, pl.ds(0, 128)], rn.at[0, pl.ds(0, 128)], n1p)
        else:
            take(("F-", k), rf.at[1])
            pb[3, 128:256, :] = (pb[3, 128:256, :].astype(F32) + rf[1].astype(F32)).astype(BF)
            send(("N-b", k), pb.at[3, pl.ds(128, 128)], rn.at[1, pl.ds(128, 128)], n1m)

    def x2(k):
        pb, rn, s2, rf2, rn2 = PB[k], RN[k], S2[k], RF2[k], RN2[k]
        take(("N", k), rn)
        for r2 in (2, 1, 3, 0):
            sl = slice(64 * r2, 64 * r2 + 64)
            tot = pb[0, sl, :].astype(F32) + rn[0, sl, :].astype(F32) + rn[1, sl, :].astype(F32)
            if r2 == 0:
                FB[k][...] = tot
            else:
                s2[r2] = tot.astype(BF)
            if k == END:
                if r2:
                    to = (rn2.at[0], rf2, rn2.at[1])[r2 - 1]
                    dev = (n2p, n2f, n2m)[r2 - 1]
                    send((("n+", "ff", "n-")[r2 - 1], k), s2.at[r2], to, dev)
            elif r2 == 2:
                send(("f+", k), s2.at[2, pl.ds(0, 32)], rf2.at[0], n2p)
                send(("f-", k), s2.at[2, pl.ds(32, 32)], rf2.at[1], n2m)
            elif r2 == 1:
                send(("n+b", k), s2.at[1, pl.ds(32, 32)], rn2.at[0, pl.ds(32, 32)], n2p)
            elif r2 == 3:
                send(("n-a", k), s2.at[3, pl.ds(0, 32)], rn2.at[1, pl.ds(0, 32)], n2m)

    def x2b(k, dirn):
        s2, rf2, rn2 = S2[k], RF2[k], RN2[k]
        if dirn == 0:
            take(("f+", k), rf2.at[0])
            s2[1, 0:32, :] = (s2[1, 0:32, :].astype(F32) + rf2[0].astype(F32)).astype(BF)
            send(("n+a", k), s2.at[1, pl.ds(0, 32)], rn2.at[0, pl.ds(0, 32)], n2p)
        else:
            take(("f-", k), rf2.at[1])
            s2[3, 32:64, :] = (s2[3, 32:64, :].astype(F32) + rf2[1].astype(F32)).astype(BF)
            send(("n-b", k), s2.at[3, pl.ds(32, 32)], rn2.at[1, pl.ds(32, 32)], n2m)

    def x3(k):
        rn2 = RN2[k]
        take(("n", k), rn2)
        tot = FB[k][...] + rn2[0].astype(F32) + rn2[1].astype(F32)
        if k == END:
            take(("ff", k), RF2[k])
            tot = tot + RF2[k][...].astype(F32)
        at = 0
        for s, a, n in CHUNKS[k]:
            OZ[zz(s), :, a : a + n] = tot[:, at : at + n]
            at += n

    def mixed(p):
        loads[f"w{p}"].wait()
        out = dot(hid[...], w[:, PAIR * p : PAIR * p + PAIR], NN).astype(BF)
        mt = dot(out, GT[...], TN).astype(BF)
        for k in range(2):
            for cc in range(2):
                o = ZBL * k + BLK * cc
                M[cc, 2 * p + k] = mt[o : o + BLK, :]
        send(("m", p), M.at[1 - c, pl.ds(2 * p, 2)], MR.at[pl.ds(2 * p, 2)], pt)

    def both(t, sl):
        return M[c, t, sl, :].astype(F32) + MR[t, sl, :].astype(F32)

    def rz(k, sub, dirn):
        take(("m",), MR)
        sl = slice(SUB * sub, SUB * sub + SUB)
        t = zz(k - 5) if dirn else zz(5 - k)
        v = both(t, sl)
        if k >= 3 or (k == 2 and sub == dirn):
            take(("z", dirn, k - 1, sub), ZR.at[dirn, k - 2, pl.ds(SUB * sub, SUB)])
            v = v + ZR[dirn, k - 2, sl, :].astype(F32)
        ZS[dirn, k - 1, sl, :] = v.astype(BF)
        send(
            ("z", dirn, k, sub),
            ZS.at[dirn, k - 1, pl.ds(SUB * sub, SUB)],
            ZR.at[dirn, k - 1, pl.ds(SUB * sub, SUB)],
            zm if dirn else zp,
        )

    def rzl():
        for dirn in range(2):
            take(("Z", dirn), ZR.at[dirn, 3])
        v = both(z, slice(0, BLK)) + ZR[0, 3].astype(F32) + ZR[1, 3].astype(F32)
        mixT[...] = v.astype(BF)

    def hg(p):
        routed = dot(GT[...], cotT[PAIR * p : PAIR * p + PAIR, :], NT).astype(BF)
        part = dot(routed, w[:, PAIR * p : PAIR * p + PAIR], NT)
        if p == 0:
            acc[...] = part
        elif p < 3:
            acc[...] += part
        else:
            hgb[...] = (acc[...] + part).astype(BF)

    mixed(0)
    x1a(0)
    ag(1, 0, 0)
    ag(1, 0, 1)
    mixed(1)
    x1a(1)
    x1b(0, 1)
    ag(1, 1, 0)
    x1b(0, 0)
    ag(1, 1, 1)
    mixed(2)
    x1a(2)
    x1o(0)
    ag(2, 0, 1)
    ag(2, 0, 0)
    mixed(3)
    x2(0)
    x1b(1, 0)
    x1o(1)
    x1b(1, 1)
    ag(2, 1, 0)
    ag(2, 1, 1)
    x1b(2, 1)
    rz(1, 1, 1)
    x1b(2, 0)
    rz(1, 0, 0)
    x1a(3)
    ag(3, 0, 1)
    ag(3, 0, 0)
    x1o(2)
    x2(1)
    ag(3, 1, 0)
    ag(3, 1, 1)
    rz(2, 1, 0)
    rz(2, 0, 1)
    x2b(0, 1)
    x2(2)
    x2b(0, 0)
    x2b(1, 0)
    x1o(3)
    x1a(4)
    x1b(3, 1)
    agl(1)
    rz(2, 1, 1)
    rz(2, 0, 0)
    agl(0)
    x2b(1, 1)
    rz(3, 1, 0)
    x1b(3, 0)
    rz(3, 0, 1)
    x1a(5)
    x1a(6)
    hg(0)
    x1b(4, 0)
    rz(3, 0, 0)
    rz(3, 1, 1)
    x1b(4, 1)
    hg(1)
    x3(0)
    x1b(5, 1)
    hg(2)
    x1b(5, 0)
    x1b(6, 0)
    x3(1)
    x1o(4)
    x1b(6, 1)
    rz(4, 1, 0)
    rz(4, 0, 0)
    rz(4, 0, 1)
    x1o(5)
    x2(3)
    x1o(6)
    rz(4, 1, 1)
    x2(4)
    x2(5)
    x2b(2, 0)
    x2(6)
    x2b(2, 1)
    x2b(3, 1)
    x2b(3, 0)
    x2b(4, 0)
    x2b(4, 1)
    x2b(5, 1)
    x2b(5, 0)
    hg(3)
    rzl()
    x3(6)
    x3(3)
    x3(4)
    x3(2)
    x3(5)
    for cp in sent[-N_SEND:]:
        cp.wait_send()


def finish(mix, hgr, blocks, mix_o, hg_o, wg_o, wgb, sem):
    first = pltpu.make_async_copy(hgr, hg_o, sem.at[4])
    second = pltpu.make_async_copy(mix, mix_o, sem.at[5])
    first.start()
    second.start()
    lane = lax.broadcasted_iota(jnp.int32, (64, 128), 1)
    rest = []
    for p in range(4):
        a, b = blocks[2 * p], pltpu.roll(blocks[2 * p + 1], 64, 1)
        o = PAIR * p
        wgb[:, o : o + 384] = a[:, 0:384]
        wgb[:, o + 384 : o + 512] = jnp.where(lane < 64, a[:, 384:512], b[:, 0:128])
        wgb[:, o + 512 : o + 896] = b[:, 128:512]
        cp = pltpu.make_async_copy(
            wgb.at[:, pl.ds(o, PAIR)], wg_o.at[:, pl.ds(o, PAIR)], sem.at[p]
        )
        cp.start()
        rest.append(cp)
    for cp in [first, second] + rest:
        cp.wait()


def body(hidden, down_weight, cotangent, expert_ids, gate_weights, row_token, tile_count):
    v = pltpu.VMEM
    scratch = [
        v((ROWS, HID), BF),
        v((HID, ROWS), BF),
        v((HID, ROWS), BF),
        v((HID, DIM), BF),
        v((8, TOK), jnp.int32),
        v((8, TOK), BF),
        v((1, ROWS), jnp.int32),
        v((ROWS, TOK), BF),
        v((DIM, TOK), BF),
    ]
    scratch += [v((ROWS, n), BF) for n in WIDTHS]
    scratch += [v((4, 256, n), BF) for n in WIDTHS]
    scratch += [v((2, 128, n), BF) for n in WIDTHS]
    scratch += [v((2, 256, n), BF) for n in WIDTHS]
    scratch += [v((4, 64, n), BF) for n in WIDTHS]
    scratch += [v((2, 32, n), BF) for n in WIDTHS[:-1]] + [v((64, WIDTHS[-1]), BF)]
    scratch += [v((2, 64, n), BF) for n in WIDTHS]
    scratch += [v((64, n), F32) for n in WIDTHS]
    scratch += [
        v((2, NZ, BLK, TOK), BF),
        v((NZ, BLK, TOK), BF),
        v((2, 4, BLK, TOK), BF),
        v((2, 4, BLK, TOK), BF),
        v((ROWS, HID), F32),
        pltpu.SemaphoreType.DMA((N_SEND,)),
        pltpu.SemaphoreType.DMA((N_RECV,)),
        pltpu.SemaphoreType.DMA((9,)),
    ]
    hbm = pl.BlockSpec(memory_space=pl.ANY)
    vm = pl.BlockSpec(memory_space=pltpu.VMEM)
    raw = pl.pallas_call(
        kernel,
        out_shape=(v((BLK, TOK), BF), v((ROWS, HID), BF), v((NZ, 64, 512), F32)),
        in_specs=[hbm] * 6 + [pl.BlockSpec(memory_space=pltpu.SMEM)],
        out_specs=(vm, vm, vm),
        scratch_shapes=scratch,
        compiler_params=pltpu.CompilerParams(
            collective_id=0, has_side_effects=True, vmem_limit_bytes=58_000_000
        ),
    )(
        hidden[0, 0],
        down_weight[0],
        cotangent.T,
        expert_ids.T,
        gate_weights.T,
        row_token[0],
        tile_count,
    )
    mixed_out, hidden_grad, weight_grad = pl.pallas_call(
        finish,
        out_shape=(
            jax.ShapeDtypeStruct((BLK, TOK), BF),
            jax.ShapeDtypeStruct((ROWS, HID), BF),
            jax.ShapeDtypeStruct((64, DIM), F32),
        ),
        in_specs=[vm] * 3,
        out_specs=(hbm,) * 3,
        scratch_shapes=[v((64, DIM), F32), pltpu.SemaphoreType.DMA((6,))],
        compiler_params=pltpu.CompilerParams(vmem_limit_bytes=4_000_000),
    )(*raw)
    return mixed_out.T, hidden_grad[None, None], weight_grad[None]


def solution(mesh):
    placed = (
        P("dp", "expert", None, None),
        P("expert", None, None),
        P("dp", "expert"),
        P("dp", None),
        P("dp", None),
        P("dp", "expert", None),
        P("dp", "expert"),
    )
    return jax.shard_map(
        body,
        mesh=mesh,
        in_specs=placed,
        out_specs=(P("dp", "expert"), P("dp", "expert", None, None), P("expert", "dp", None)),
        check_vma=False,
    )
```
